512 devices in a mesh: layer: 4 (over y_hi, core), feat: 128 (over y_lo, z, x).
Axes of the slice: x: 4, y: 4 (y_hi: 2, y_lo: 2; y = y_hi * 2 + y_lo), z: 16, core: 2. Of those that a mesh axis runs over, the one named last changes fastest.
Arguments:
- resid_stream: bfloat16 [128, 4, 2304], P('feat', 'layer'), may hold values from -6 to 6
- enc_mantissa: bfloat16 [4, 2304, 16384], P('layer', None, 'feat'), may hold values from -96 to 96
- enc_exponent: int32 [4, 18, 128], P('layer', None, 'feat'), may hold values from -11 to -10
- enc_bias: float32 [4, 16384], P('layer', 'feat'), may hold values from -3 to 3
- dec_weight: bfloat16 [10, 16384, 2304], P(None, 'feat', 'layer'), may hold values from -0.046875 to 0.046875
- dec_bias: float32 [4, 2304], P('layer'), may hold values from -3 to 3
Outputs:
- recon: bfloat16 [128, 4, 2304], P('feat', 'layer')
The draws below stay inside these ranges and needn't reach their ends.
All inputs are finite; a program needn't handle non-finite values.
Results may differ from the reference program's by a relative error of at most 0.0044.
Values may be sent and summed in bfloat16 or wider, within the bound.
A program may use at most 64 MiB of HBM per device.

```python
import jax
import jax.numpy as jnp

D = 2304
F = 16384
LAYERS = 4
BLK = 128
TOKENS = 128
PAIRS = 10


def place_ends(array, own_key, low, high):
    place = [jax.random.randint(jax.random.fold_in(own_key, axis), (), 0, length) for axis, length in enumerate(array.shape)]
    widest = array.shape.index(max(array.shape))
    neighbour = place[:widest] + [(place[widest] + 1) % array.shape[widest]] + place[widest + 1:]
    return array.at[tuple(place)].set(low).at[tuple(neighbour)].set(high)


def shard_levels(stream_key, dims, split, low, largest):
    level = 1.0
    for axis_at, blocks in split:
        steps = jax.random.uniform(jax.random.fold_in(jax.random.fold_in(stream_key, 6), axis_at), (blocks,), jnp.float32, low / len(split), largest / len(split))
        level = level * jnp.repeat(jnp.exp(steps), dims[axis_at] // blocks).reshape((-1,) + (1,) * (len(dims) - 1 - axis_at))
    return level


def scatter_about(stream_key, shape, scale, reach, cuts=(), held_as=jnp.bfloat16):
    result = jax.random.normal(stream_key, shape, jnp.float32) * scale
    if len(cuts) > 0:
        result = shard_levels(stream_key, shape, cuts, -0.22, 0.18) * result
    return jnp.clip(result, min=-reach, max=reach).astype(held_as)


def setup_inputs(seed: int = 0) -> dict:
    key_list = jax.random.split(jax.random.key(seed), 7)
    return {
        "resid_stream": scatter_about(key_list[0], (TOKENS, LAYERS, D), 1.0, 6.0, ((0, 128), (1, 4))),
        "enc_mantissa": scatter_about(key_list[1], (LAYERS, D, F), 16.0, 96.0, ((0, 4), (2, 128))),
        "enc_exponent": place_ends(jax.random.randint(key_list[2], (LAYERS, D // BLK, F // BLK), -11, -9), jax.random.fold_in(key_list[2], 1), -11, (-9) - 1).astype(jnp.int32),
        "enc_bias": scatter_about(key_list[3], (LAYERS, F), 0.5, 3.0, ((0, 4), (1, 128)), jnp.float32),
        "dec_weight": scatter_about(key_list[4], (PAIRS, F, D), F ** -0.5, 0.046875, ((1, 128), (2, 4))),
        "dec_bias": scatter_about(key_list[5], (LAYERS, D), 0.5, 3.0, ((0, 4),), jnp.float32),
    }


def dequantize(mantissa, exponent):
    scales = jnp.exp2(exponent.astype(jnp.float32))
    blocks = mantissa.astype(jnp.float32).reshape(D // BLK, BLK, F // BLK, BLK)
    return (blocks * scales[:, None, :, None]).reshape(D, F).astype(jnp.bfloat16)


def reference(resid_stream, enc_mantissa, enc_exponent, enc_bias, dec_weight, dec_bias):
    latents = []
    for layer_index in range(LAYERS):
        weight = dequantize(enc_mantissa[layer_index], enc_exponent[layer_index])
        pre_act = jnp.dot(resid_stream[:, layer_index, :], weight, preferred_element_type=jnp.float32)
        latents.append(jnp.maximum(pre_act + enc_bias[layer_index][None, :], 0.0).astype(jnp.bfloat16))
    outputs = []
    for target in range(LAYERS):
        total = jnp.zeros((TOKENS, D), jnp.float32)
        for source in range(target + 1):
            pair_index = target * (target + 1) // 2 + source
            total = total + jnp.dot(latents[source], dec_weight[pair_index], preferred_element_type=jnp.float32)
        outputs.append((total + dec_bias[target][None, :]).astype(jnp.bfloat16))
    return jnp.stack(outputs, axis=1)
```

```python
import jax
import jax.numpy as jnp
from jax import lax
from jax.experimental import pallas as pl
from jax.experimental.pallas import tpu as pltpu
from jax.sharding import PartitionSpec as P

LY = 4
NX = 4
NP = 8
NZ = 16
BLK = 128
PITCH = 24
MESH = pl.DeviceIdType.MESH


def pow2(exponent):
    down = -exponent
    scale = jnp.ones(exponent.shape, jnp.float32)
    for bit in range(7):
        scale = scale * jnp.where((down & (1 << bit)) != 0, jnp.float32(2.0 ** -(1 << bit)), jnp.float32(1.0))
    return scale


def kernel(
    x_ref, m_ref, e_ref, eb_ref, d_ref, db_ref, out_ref,
    w_v, d_v, own, rows, stage, xg, lat, part, rs1, stage2, sb, rz,
    loc_sem, zs, zr, ps, pr, ls, lr, rs_s, rs_r, fs, fr,
):
    layer = lax.axis_index("layer")
    feat = lax.axis_index("feat")
    y_lo = feat // (NZ * NX)
    z = (feat // NX) % NZ
    x = feat % NX
    p = y_lo * NX + x
    width = x_ref.shape[1]
    blocks = width // BLK
    cols = d_ref.shape[1]
    chunks = part.shape[3] // BLK

    def feat_of(place, zz):
        return (place // NX) * (NZ * NX) + zz * NX + place % NX

    load_w = pltpu.make_async_copy(m_ref, w_v, loc_sem.at[0])
    load_d = pltpu.make_async_copy(d_ref, d_v, loc_sem.at[1])
    load_w.start()
    load_d.start()

    barrier = pltpu.get_barrier_semaphore()

    @pl.loop(1, NZ)
    def _(k):
        pl.semaphore_signal(barrier, inc=1, device_id=(layer, feat_of(p, (z + k) % NZ)), device_id_type=MESH)

    @pl.loop(1, LY * NP)
    def _(k):
        q = (layer * NP + p + k) % (LY * NP)
        pl.semaphore_signal(barrier, inc=1, device_id=(q // NP, feat_of(q % NP, z)), device_id_type=MESH)

    for b in range(blocks):
        own[b : b + 1, :] = x_ref[0:1, b * BLK : (b + 1) * BLK].astype(jnp.float32)
    rows[z] = own[0:blocks, :].astype(jnp.bfloat16)
    for t in range(LY):
        part[t, :, :, 512:640] = jnp.zeros((NP, NZ, 128), jnp.bfloat16)

    pl.semaphore_wait(barrier, (NZ - 1) + (LY * NP - 1))

    def z_copy(slot, other):
        return pltpu.make_async_remote_copy(
            src_ref=rows.at[z], dst_ref=rows.at[slot], send_sem=zs.at[other], recv_sem=zr.at[slot],
            device_id=(layer, feat_of(p, other)), device_id_type=MESH,
        )

    @pl.loop(1, NZ)
    def _(k):
        z_copy(z, (z + k) % NZ).start()

    load_w.wait()
    scales = pow2(e_ref[0:1, :])
    for b in range(blocks):
        piece = slice(b * BLK, (b + 1) * BLK)
        w_v[piece, :] = (w_v[piece, :].astype(jnp.float32) * scales[0:1, b : b + 1]).astype(jnp.bfloat16)

    @pl.loop(1, NZ)
    def _(k):
        other = (z + k) % NZ
        z_copy(other, other).wait_recv()

    for zz in range(NZ):
        stage[zz * PITCH : zz * PITCH + blocks, :] = rows[zz].astype(jnp.float32)
    for b in range(blocks):
        xg[p, :, b * BLK : (b + 1) * BLK] = stage[pl.ds(b, NZ, stride=PITCH), :].astype(jnp.bfloat16)

    def p_copy(slot, other):
        return pltpu.make_async_remote_copy(
            src_ref=xg.at[p], dst_ref=xg.at[slot], send_sem=ps.at[other], recv_sem=pr.at[slot],
            device_id=(layer, feat_of(other, z)), device_id_type=MESH,
        )

    @pl.loop(1, NP)
    def _(k):
        p_copy(p, (p + k) % NP).start()

    @pl.loop(1, NP)
    def _(k):
        other = (p + k) % NP
        p_copy(other, other).wait_recv()

    tokens = NP * NZ
    pre = jnp.dot(xg[...].reshape(tokens, width), w_v[...], preferred_element_type=jnp.float32)
    lat[layer] = jnp.maximum(pre + eb_ref[...], 0.0).astype(jnp.bfloat16)

    def l_copy(slot, other):
        return pltpu.make_async_remote_copy(
            src_ref=lat.at[layer], dst_ref=lat.at[slot], send_sem=ls.at[other], recv_sem=lr.at[slot],
            device_id=(other, feat), device_id_type=MESH,
        )

    @pl.loop(1, LY)
    def _(k):
        l_copy(layer, (layer + k) % LY).start()

    load_d.wait()

    @pl.loop(1, LY)
    def _(k):
        other = (layer + k) % LY
        l_copy(other, other).wait_recv()

    for t in range(LY):
        total = jnp.zeros((tokens, cols), jnp.float32)
        for s in range(t + 1):
            total = total + lax.dot_general(
                lat[s], d_v[t * (t + 1) // 2 + s], (((1,), (1,)), ((), ())), preferred_element_type=jnp.float32
            )
        part[t, :, :, 0:cols] = total.reshape(NP, NZ, cols).astype(jnp.bfloat16)

    def r_copy(src, slot, other):
        return pltpu.make_async_remote_copy(
            src_ref=part.at[src // NP, src % NP], dst_ref=rs1.at[slot // NP, slot % NP],
            send_sem=rs_s.at[other], recv_sem=rs_r.at[slot],
            device_id=(other // NP, feat_of(other % NP, z)), device_id_type=MESH,
        )

    mine = layer * NP + p

    @pl.loop(1, LY * NP)
    def _(k):
        q = (mine + k) % (LY * NP)
        r_copy(q, mine, q).start()

    rs1[layer, p] = part[layer, p]

    @pl.loop(1, LY * NP)
    def _(k):
        q = (mine + k) % (LY * NP)
        r_copy(q, q, q).wait_recv()

    for s in range(LY):
        total = rs1[s, 0].astype(jnp.float32)
        for place in range(1, NP):
            total = total + rs1[s, place].astype(jnp.float32)
        for c in range(chunks):
            stage2[pl.ds(s * chunks + c, NZ, stride=PITCH), :] = total[:, c * BLK : (c + 1) * BLK]
    for zz in range(NZ):
        sb[zz] = stage2[zz * PITCH : zz * PITCH + LY * chunks, :].astype(jnp.bfloat16)

    def f_copy(slot, other):
        return pltpu.make_async_remote_copy(
            src_ref=sb.at[other], dst_ref=rz.at[slot], send_sem=fs.at[other], recv_sem=fr.at[slot],
            device_id=(layer, feat_of(p, other)), device_id_type=MESH,
        )

    @pl.loop(1, NZ)
    def _(k):
        f_copy(z, (z + k) % NZ).start()

    rz[z] = sb[z]

    @pl.loop(1, NZ)
    def _(k):
        other = (z + k) % NZ
        f_copy(other, other).wait_recv()

    total = rz[0].astype(jnp.float32)
    for zz in range(1, NZ):
        total = total + rz[zz].astype(jnp.float32)

    half = BLK // 2
    low = lax.broadcasted_iota(jnp.int32, (1, BLK), 1) < half
    turned = pltpu.roll(total, half, 1)
    at = 0
    for pair in range(LY // 2):
        even, odd = pair * 2 * chunks, (pair * 2 + 1) * chunks
        pieces = [total[even + c : even + c + 1, :] for c in range(chunks - 1)]
        pieces.append(jnp.where(low, total[even + chunks - 1 : even + chunks, :], turned[odd : odd + 1, :]))
        for c in range(1, chunks):
            pieces.append(jnp.where(low, turned[odd + c - 1 : odd + c, :], turned[odd + c : odd + c + 1, :]))
        for piece in pieces:
            out_ref[0:1, at : at + BLK] = (piece + db_ref[0:1, at : at + BLK]).astype(jnp.bfloat16)
            at += BLK

    @pl.loop(1, NZ)
    def _(k):
        other = (z + k) % NZ
        z_copy(z, other).wait_send()
        f_copy(z, other).wait_send()

    @pl.loop(1, NP)
    def _(k):
        p_copy(p, (p + k) % NP).wait_send()

    @pl.loop(1, LY)
    def _(k):
        l_copy(layer, (layer + k) % LY).wait_send()

    @pl.loop(1, LY * NP)
    def _(k):
        q = (mine + k) % (LY * NP)
        r_copy(q, mine, q).wait_send()


def shards(resid_stream, enc_mantissa, enc_exponent, enc_bias, dec_weight, dec_bias):
    width = resid_stream.shape[2]
    feats = enc_mantissa.shape[2]
    pairs, _, cols = dec_weight.shape
    blocks = width // BLK
    padded = (cols + BLK - 1) // BLK * BLK
    vm = pl.BlockSpec(memory_space=pltpu.VMEM)
    hbm = pl.BlockSpec(memory_space=pl.ANY)
    dma = pltpu.SemaphoreType.DMA
    bf, f32 = jnp.bfloat16, jnp.float32
    out = pl.pallas_call(
        kernel,
        out_shape=jax.ShapeDtypeStruct((1, width), bf),
        in_specs=[vm, hbm, vm, vm, hbm, vm],
        out_specs=vm,
        scratch_shapes=[
            pltpu.VMEM((width, feats), bf),
            pltpu.VMEM((pairs, cols, feats), bf),
            pltpu.VMEM((PITCH, BLK), f32),
            pltpu.VMEM((NZ, blocks, BLK), bf),
            pltpu.VMEM((NZ * PITCH, BLK), f32),
            pltpu.VMEM((NP, NZ, width), bf),
            pltpu.VMEM((LY, NP * NZ, feats), bf),
            pltpu.VMEM((LY, NP, NZ, padded), bf),
            pltpu.VMEM((LY, NP, NZ, padded), bf),
            pltpu.VMEM((NZ * PITCH, BLK), f32),
            pltpu.VMEM((NZ, LY * padded // BLK, BLK), bf),
            pltpu.VMEM((NZ, LY * padded // BLK, BLK), bf),
            dma((2,)),
            dma((NZ,)), dma((NZ,)),
            dma((NP,)), dma((NP,)),
            dma((LY,)), dma((LY,)),
            dma((LY * NP,)), dma((LY * NP,)),
            dma((NZ,)), dma((NZ,)),
        ],
        compiler_params=pltpu.CompilerParams(collective_id=0, has_side_effects=True),
    )(
        resid_stream.reshape(1, width),
        enc_mantissa[0],
        enc_exponent.reshape(1, blocks),
        enc_bias,
        dec_weight.transpose(0, 2, 1),
        dec_bias,
    )
    return out[:, None, :]


def solution(mesh):
    in_specs = (
        P("feat", "layer", None),
        P("layer", None, "feat"),
        P("layer", None, "feat"),
        P("layer", "feat"),
        P(None, "feat", "layer"),
        P("layer", None),
    )
    out_specs = P("feat", "layer", None)
    return jax.shard_map(shards, mesh=mesh, in_specs=in_specs, out_specs=out_specs, check_vma=False)
```

```python
import jax
import jax.numpy as jnp
from jax import lax
from jax.experimental import pallas as pl
from jax.experimental.pallas import tpu as pltpu
from jax.sharding import PartitionSpec as P

LY = 4
NX = 4
NP = 8
NZ = 16
BLK = 128
PITCH = 24
MESH = pl.DeviceIdType.MESH
RING = (2, 1, 3, 0)
PLANE = sorted(((dy, dx) for dy in RING for dx in RING), key=lambda s: -(min(s[0], 4 - s[0]) + min(s[1], 4 - s[1])))


def pow2(exponent):
    down = -exponent
    scale = jnp.ones(exponent.shape, jnp.float32)
    for bit in range(7):
        scale = scale * jnp.where((down & (1 << bit)) != 0, jnp.float32(2.0 ** -(1 << bit)), jnp.float32(1.0))
    return scale


def kernel(
    x_ref, m_ref, e_ref, eb_ref, d_ref, db_ref, out_ref,
    w_v, d_v, own, rows, stage, xg, lat, part, rs1, stage2, sb, rz,
    loc_sem, zs, zr, ps, pr, ls, lr, rs_s, rs_r, fs, fr,
):
    layer = lax.axis_index("layer")
    feat = lax.axis_index("feat")
    y_lo = feat // (NZ * NX)
    z = (feat // NX) % NZ
    x = feat % NX
    p = y_lo * NX + x
    width = x_ref.shape[1]
    blocks = width // BLK
    cols = d_ref.shape[1]
    chunks = part.shape[3] // BLK

    def feat_of(place, zz):
        return (place // NX) * (NZ * NX) + zz * NX + place % NX

    def far_first(send):
        send((z + NZ // 2) % NZ)

        @pl.loop(1, NZ // 2)
        def _(k):
            send((z + NZ // 2 - k) % NZ)
            send((z + NZ // 2 + k) % NZ)

    load_w = pltpu.make_async_copy(m_ref, w_v, loc_sem.at[0])
    load_d = pltpu.make_async_copy(d_ref, d_v, loc_sem.at[1])
    load_w.start()
    load_d.start()

    barrier = pltpu.get_barrier_semaphore()

    @pl.loop(1, NZ)
    def _(k):
        pl.semaphore_signal(barrier, inc=1, device_id=(layer, feat_of(p, (z + k) % NZ)), device_id_type=MESH)

    @pl.loop(1, LY * NP)
    def _(k):
        q = (layer * NP + p + k) % (LY * NP)
        pl.semaphore_signal(barrier, inc=1, device_id=(q // NP, feat_of(q % NP, z)), device_id_type=MESH)

    for b in range(blocks):
        own[b : b + 1, :] = x_ref[0:1, b * BLK : (b + 1) * BLK].astype(jnp.float32)
    rows[z] = own[0:blocks, :].astype(jnp.bfloat16)
    for t in range(LY):
        part[t, :, :, 512:640] = jnp.zeros((NP, NZ, 128), jnp.bfloat16)

    pl.semaphore_wait(barrier, (NZ - 1) + (LY * NP - 1))

    def z_copy(slot, other):
        return pltpu.make_async_remote_copy(
            src_ref=rows.at[z], dst_ref=rows.at[slot], send_sem=zs.at[other], recv_sem=zr.at[slot],
            device_id=(layer, feat_of(p, other)), device_id_type=MESH,
        )

    far_first(lambda other: z_copy(z, other).start())

    load_w.wait()
    scales = pow2(e_ref[0:1, :])
    for b in range(blocks):
        piece = slice(b * BLK, (b + 1) * BLK)
        w_v[piece, :] = (w_v[piece, :].astype(jnp.float32) * scales[0:1, b : b + 1]).astype(jnp.bfloat16)

    @pl.loop(1, NZ)
    def _(k):
        other = (z + k) % NZ
        z_copy(other, other).wait_recv()

    for zz in range(NZ):
        stage[zz * PITCH : zz * PITCH + blocks, :] = rows[zz].astype(jnp.float32)
    for b in range(blocks):
        xg[p, :, b * BLK : (b + 1) * BLK] = stage[pl.ds(b, NZ, stride=PITCH), :].astype(jnp.bfloat16)

    def p_copy(slot, other):
        return pltpu.make_async_remote_copy(
            src_ref=xg.at[p], dst_ref=xg.at[slot], send_sem=ps.at[other], recv_sem=pr.at[slot],
            device_id=(layer, feat_of(other, z)), device_id_type=MESH,
        )

    for dy in (1, 0):
        for dx in RING:
            if dy or dx:
                p_copy(p, (y_lo + dy) % 2 * NX + (x + dx) % NX).start()

    @pl.loop(1, NP)
    def _(k):
        other = (p + k) % NP
        p_copy(other, other).wait_recv()

    tokens = NP * NZ
    pre = jnp.dot(xg[...].reshape(tokens, width), w_v[...], preferred_element_type=jnp.float32)
    lat[layer] = jnp.maximum(pre + eb_ref[...], 0.0).astype(jnp.bfloat16)

    def l_copy(slot, other):
        return pltpu.make_async_remote_copy(
            src_ref=lat.at[layer], dst_ref=lat.at[slot], send_sem=ls.at[other], recv_sem=lr.at[slot],
            device_id=(other, feat), device_id_type=MESH,
        )

    @pl.loop(1, LY)
    def _(k):
        l_copy(layer, (layer + k) % LY).start()

    load_d.wait()

    @pl.loop(1, LY)
    def _(k):
        other = (layer + k) % LY
        l_copy(other, other).wait_recv()

    for t in range(LY):
        total = jnp.zeros((tokens, cols), jnp.float32)
        for s in range(t + 1):
            total = total + lax.dot_general(
                lat[s], d_v[t * (t + 1) // 2 + s], (((1,), (1,)), ((), ())), preferred_element_type=jnp.float32
            )
        part[t, :, :, 0:cols] = total.reshape(NP, NZ, cols).astype(jnp.bfloat16)

    def r_copy(src, slot, other):
        return pltpu.make_async_remote_copy(
            src_ref=part.at[src // NP, src % NP], dst_ref=rs1.at[slot // NP, slot % NP],
            send_sem=rs_s.at[other], recv_sem=rs_r.at[slot],
            device_id=(other // NP, feat_of(other % NP, z)), device_id_type=MESH,
        )

    mine = layer * NP + p

    y, core = layer // 2 * 2 + y_lo, layer % 2
    for dy, dx in PLANE:
        for dc in (1, 0):
            if dy or dx or dc:
                to_y = (y + dy) % 4
                to = (to_y // 2 * 2 + (core + dc) % 2) * NP + to_y % 2 * NX + (x + dx) % NX
                r_copy(to, mine, to).start()

    rs1[layer, p] = part[layer, p]

    @pl.loop(1, LY * NP)
    def _(k):
        q = (mine + k) % (LY * NP)
        r_copy(q, q, q).wait_recv()

    for s in range(LY):
        total = rs1[s, 0].astype(jnp.float32)
        for place in range(1, NP):
            total = total + rs1[s, place].astype(jnp.float32)
        for c in range(chunks):
            stage2[pl.ds(s * chunks + c, NZ, stride=PITCH), :] = total[:, c * BLK : (c + 1) * BLK]
    for zz in range(NZ):
        sb[zz] = stage2[zz * PITCH : zz * PITCH + LY * chunks, :].astype(jnp.bfloat16)

    def f_copy(slot, other):
        return pltpu.make_async_remote_copy(
            src_ref=sb.at[other], dst_ref=rz.at[slot], send_sem=fs.at[other], recv_sem=fr.at[slot],
            device_id=(layer, feat_of(p, other)), device_id_type=MESH,
        )

    far_first(lambda other: f_copy(z, other).start())

    rz[z] = sb[z]

    @pl.loop(1, NZ)
    def _(k):
        other = (z + k) % NZ
        f_copy(other, other).wait_recv()

    total = rz[0].astype(jnp.float32)
    for zz in range(1, NZ):
        total = total + rz[zz].astype(jnp.float32)

    half = BLK // 2
    low = lax.broadcasted_iota(jnp.int32, (1, BLK), 1) < half
    turned = pltpu.roll(total, half, 1)
    at = 0
    for pair in range(LY // 2):
        even, odd = pair * 2 * chunks, (pair * 2 + 1) * chunks
        pieces = [total[even + c : even + c + 1, :] for c in range(chunks - 1)]
        pieces.append(jnp.where(low, total[even + chunks - 1 : even + chunks, :], turned[odd : odd + 1, :]))
        for c in range(1, chunks):
            pieces.append(jnp.where(low, turned[odd + c - 1 : odd + c, :], turned[odd + c : odd + c + 1, :]))
        for piece in pieces:
            out_ref[0:1, at : at + BLK] = (piece + db_ref[0:1, at : at + BLK]).astype(jnp.bfloat16)
            at += BLK

    @pl.loop(1, NZ)
    def _(k):
        other = (z + k) % NZ
        z_copy(z, other).wait_send()
        f_copy(z, other).wait_send()

    @pl.loop(1, NP)
    def _(k):
        p_copy(p, (p + k) % NP).wait_send()

    @pl.loop(1, LY)
    def _(k):
        l_copy(layer, (layer + k) % LY).wait_send()

    @pl.loop(1, LY * NP)
    def _(k):
        q = (mine + k) % (LY * NP)
        r_copy(q, mine, q).wait_send()


def shards(resid_stream, enc_mantissa, enc_exponent, enc_bias, dec_weight, dec_bias):
    width = resid_stream.shape[2]
    feats = enc_mantissa.shape[2]
    pairs, _, cols = dec_weight.shape
    blocks = width // BLK
    padded = (cols + BLK - 1) // BLK * BLK
    vm = pl.BlockSpec(memory_space=pltpu.VMEM)
    hbm = pl.BlockSpec(memory_space=pl.ANY)
    dma = pltpu.SemaphoreType.DMA
    bf, f32 = jnp.bfloat16, jnp.float32
    out = pl.pallas_call(
        kernel,
        out_shape=jax.ShapeDtypeStruct((1, width), bf),
        in_specs=[vm, hbm, vm, vm, hbm, vm],
        out_specs=vm,
        scratch_shapes=[
            pltpu.VMEM((width, feats), bf),
            pltpu.VMEM((pairs, cols, feats), bf),
            pltpu.VMEM((PITCH, BLK), f32),
            pltpu.VMEM((NZ, blocks, BLK), bf),
            pltpu.VMEM((NZ * PITCH, BLK), f32),
            pltpu.VMEM((NP, NZ, width), bf),
            pltpu.VMEM((LY, NP * NZ, feats), bf),
            pltpu.VMEM((LY, NP, NZ, padded), bf),
            pltpu.VMEM((LY, NP, NZ, padded), bf),
            pltpu.VMEM((NZ * PITCH, BLK), f32),
            pltpu.VMEM((NZ, LY * padded // BLK, BLK), bf),
            pltpu.VMEM((NZ, LY * padded // BLK, BLK), bf),
            dma((2,)),
            dma((NZ,)), dma((NZ,)),
            dma((NP,)), dma((NP,)),
            dma((LY,)), dma((LY,)),
            dma((LY * NP,)), dma((LY * NP,)),
            dma((NZ,)), dma((NZ,)),
        ],
        compiler_params=pltpu.CompilerParams(collective_id=0, has_side_effects=True),
    )(
        resid_stream.reshape(1, width),
        enc_mantissa[0],
        enc_exponent.reshape(1, blocks),
        enc_bias,
        dec_weight.transpose(0, 2, 1),
        dec_bias,
    )
    return out[:, None, :]


def solution(mesh):
    in_specs = (
        P("feat", "layer", None),
        P("layer", None, "feat"),
        P("layer", None, "feat"),
        P("layer", "feat"),
        P(None, "feat", "layer"),
        P("layer", None),
    )
    out_specs = P("feat", "layer", None)
    return jax.shard_map(shards, mesh=mesh, in_specs=in_specs, out_specs=out_specs, check_vma=False)
```

```python
import jax
import jax.numpy as jnp
from jax import lax
from jax.experimental import pallas as pl
from jax.experimental.pallas import tpu as pltpu
from jax.sharding import PartitionSpec as P

LY = 4
NX = 4
NP = 8
NZ = 16
BLK = 128
PITCH = 24
MESH = pl.DeviceIdType.MESH
GROUP = 8
REACH = 4
Z_STEPS = (-4, 4, -3, 3, -2, 2, -1, 1)
PASSED = (-1, 1, -2, 2, -3, 3, -4)
RING = (2, 1, 3, 0)
PLANE = sorted(
    ((dy, dx, dc) for dy in RING for dx in RING for dc in (1, 0) if dy or dx or dc),
    key=lambda s: -(min(s[0], 4 - s[0]) + min(s[1], 4 - s[1])),
)


def pow2(exponent):
    down = -exponent
    scale = jnp.ones(exponent.shape, jnp.float32)
    for bit in range(7):
        scale = scale * jnp.where((down & (1 << bit)) != 0, jnp.float32(2.0 ** -(1 << bit)), jnp.float32(1.0))
    return scale


def kernel(
    x_ref, m_ref, e_ref, eb_ref, d_ref, db_ref, out_ref,
    w_v, d_v, own, rows, stage, xg, lat, part, rs1, stage2, sb, rz,
    loc_sem, zs, zf, zr, ps, pr, ls, lr, rs_s, rs_r, fs, fr,
):
    layer = lax.axis_index("layer")
    feat = lax.axis_index("feat")
    y_lo = feat // (NZ * NX)
    z = (feat // NX) % NZ
    x = feat % NX
    p = y_lo * NX + x
    y, core = layer // 2 * 2 + y_lo, layer % 2
    mine = layer * NP + p
    width = x_ref.shape[1]
    blocks = width // BLK
    cols = d_ref.shape[1]
    chunks = part.shape[4] // BLK

    def feat_of(place, zz):
        return (place // NX) * (NZ * NX) + zz * NX + place % NX

    def along(step):
        return (z + step + NZ) % NZ

    def row_of(group, i):
        return (z + NZ - REACH + GROUP * group + i) % NZ

    def plane_to(dy, dx, dc):
        to_y = (y + dy) % 4
        return (to_y // 2 * 2 + (core + dc) % 2) * NP + to_y % 2 * NX + (x + dx) % NX

    load_w = pltpu.make_async_copy(m_ref, w_v, loc_sem.at[0])
    load_d = pltpu.make_async_copy(d_ref, d_v, loc_sem.at[1])
    load_w.start()
    load_d.start()

    barrier = pltpu.get_barrier_semaphore()
    for step in Z_STEPS:
        pl.semaphore_signal(barrier, inc=1, device_id=(layer, feat_of(p, along(step))), device_id_type=MESH)
    for dy, dx, dc in PLANE:
        to = plane_to(dy, dx, dc)
        pl.semaphore_signal(barrier, inc=1, device_id=(to // NP, feat_of(to % NP, z)), device_id_type=MESH)

    for b in range(blocks):
        own[b : b + 1, :] = x_ref[0:1, b * BLK : (b + 1) * BLK].astype(jnp.float32)
    rows[z] = own[0:blocks, :].astype(jnp.bfloat16)
    for g in range(2):
        for t in range(LY):
            part[g, t, :, :, 512:640] = jnp.zeros((NP, GROUP, 128), jnp.bfloat16)

    pl.semaphore_wait(barrier, len(Z_STEPS) + len(PLANE))

    def z_copy(row, sems, sem, step):
        return pltpu.make_async_remote_copy(
            src_ref=rows.at[row], dst_ref=rows.at[row], send_sem=sems.at[sem], recv_sem=zr.at[row],
            device_id=(layer, feat_of(p, along(step))), device_id_type=MESH,
        )

    for n, step in enumerate(Z_STEPS):
        z_copy(z, zs, n, step).start()

    load_w.wait()
    scales = pow2(e_ref[0:1, :])
    for b in range(blocks):
        piece = slice(b * BLK, (b + 1) * BLK)
        w_v[piece, :] = (w_v[piece, :].astype(jnp.float32) * scales[0:1, b : b + 1]).astype(jnp.bfloat16)

    def arrived(step):
        z_copy(along(step), zs, 0, 1).wait_recv()

    for n, step in enumerate(PASSED):
        arrived(step)
        z_copy(along(step), zf, n, REACH if step < 0 else -REACH).start()

    def p_copy(group, slot, other):
        return pltpu.make_async_remote_copy(
            src_ref=xg.at[group, p], dst_ref=xg.at[group, slot],
            send_sem=ps.at[group, other], recv_sem=pr.at[group, slot],
            device_id=(layer, feat_of(other, z)), device_id_type=MESH,
        )

    def spread(g):
        for i in range(GROUP):
            stage[i * PITCH : i * PITCH + blocks, :] = rows[row_of(g, i)].astype(jnp.float32)
        for b in range(blocks):
            xg[g, p, :, b * BLK : (b + 1) * BLK] = stage[pl.ds(b, GROUP, stride=PITCH), :].astype(jnp.bfloat16)
        for dy in (1, 0):
            for dx in RING:
                if dy or dx:
                    p_copy(g, p, (y_lo + dy) % 2 * NX + (x + dx) % NX).start()

    spread(0)
    for step in range(REACH, REACH + GROUP):
        arrived(step)
    spread(1)

    def l_copy(group, slot, other):
        return pltpu.make_async_remote_copy(
            src_ref=lat.at[layer, group], dst_ref=lat.at[slot, group],
            send_sem=ls.at[group, other], recv_sem=lr.at[group, slot],
            device_id=(other, feat), device_id_type=MESH,
        )

    tokens = NP * GROUP

    def encode(g):
        @pl.loop(1, NP)
        def _(k):
            other = (p + k) % NP
            p_copy(g, other, other).wait_recv()

        pre = jnp.dot(xg[g].reshape(tokens, width), w_v[...], preferred_element_type=jnp.float32)
        lat[layer, g] = jnp.maximum(pre + eb_ref[...], 0.0).astype(jnp.bfloat16)
        for k in (2, 3, 1):
            l_copy(g, layer, (layer + k) % LY).start()

    def r_copy(group, src, slot, other):
        return pltpu.make_async_remote_copy(
            src_ref=part.at[group, src // NP, src % NP], dst_ref=rs1.at[group, slot // NP, slot % NP],
            send_sem=rs_s.at[group, other], recv_sem=rs_r.at[group, slot],
            device_id=(other // NP, feat_of(other % NP, z)), device_id_type=MESH,
        )

    def decode(g):
        @pl.loop(1, LY)
        def _(k):
            other = (layer + k) % LY
            l_copy(g, other, other).wait_recv()

        for t in range(LY):
            total = jnp.zeros((tokens, cols), jnp.float32)
            for s in range(t + 1):
                total = total + lax.dot_general(
                    lat[s, g], d_v[t * (t + 1) // 2 + s], (((1,), (1,)), ((), ())),
                    preferred_element_type=jnp.float32,
                )
            part[g, t, :, :, 0:cols] = total.reshape(NP, GROUP, cols).astype(jnp.bfloat16)
        for dy, dx, dc in PLANE:
            to = plane_to(dy, dx, dc)
            r_copy(g, to, mine, to).start()
        rs1[g, layer, p] = part[g, layer, p]

    encode(0)
    load_d.wait()
    decode(0)
    encode(1)
    decode(1)

    def f_copy(row, slot):
        return pltpu.make_async_remote_copy(
            src_ref=sb.at[row], dst_ref=rz.at[slot], send_sem=fs.at[row], recv_sem=fr.at[slot],
            device_id=(layer, feat_of(p, row)), device_id_type=MESH,
        )

    def gathered(g):
        @pl.loop(1, LY * NP)
        def _(k):
            q = (mine + k) % (LY * NP)
            r_copy(g, q, q, q).wait_recv()

        for s in range(LY):
            total = rs1[g, s, 0].astype(jnp.float32)
            for place in range(1, NP):
                total = total + rs1[g, s, place].astype(jnp.float32)
            for c in range(chunks):
                stage2[pl.ds(s * chunks + c, GROUP, stride=PITCH), :] = total[:, c * BLK : (c + 1) * BLK]
        for i in range(GROUP):
            sb[row_of(g, i)] = stage2[i * PITCH : i * PITCH + LY * chunks, :].astype(jnp.bfloat16)

    gathered(0)
    for step in (-4, 3, -3, 2, -2, 1, -1):
        f_copy(along(step), z).start()
    rz[z] = sb[z]
    gathered(1)
    for step in (8, 7, 9, 6, 10, 5, 11, 4):
        f_copy(along(step), z).start()

    @pl.loop(1, NZ)
    def _(k):
        other = (z + k) % NZ
        f_copy(other, other).wait_recv()

    total = rz[0].astype(jnp.float32)
    for zz in range(1, NZ):
        total = total + rz[zz].astype(jnp.float32)

    half = BLK // 2
    low = lax.broadcasted_iota(jnp.int32, (1, BLK), 1) < half
    turned = pltpu.roll(total, half, 1)
    at = 0
    for pair in range(LY // 2):
        even, odd = pair * 2 * chunks, (pair * 2 + 1) * chunks
        pieces = [total[even + c : even + c + 1, :] for c in range(chunks - 1)]
        pieces.append(jnp.where(low, total[even + chunks - 1 : even + chunks, :], turned[odd : odd + 1, :]))
        for c in range(1, chunks):
            pieces.append(jnp.where(low, turned[odd + c - 1 : odd + c, :], turned[odd + c : odd + c + 1, :]))
        for piece in pieces:
            out_ref[0:1, at : at + BLK] = (piece + db_ref[0:1, at : at + BLK]).astype(jnp.bfloat16)
            at += BLK

    for n, step in enumerate(Z_STEPS):
        z_copy(z, zs, n, step).wait_send()
    for n, step in enumerate(PASSED):
        z_copy(along(step), zf, n, REACH if step < 0 else -REACH).wait_send()

    @pl.loop(1, NZ)
    def _(k):
        f_copy((z + k) % NZ, z).wait_send()

    for g in range(2):
        @pl.loop(1, NP)
        def _(k):
            p_copy(g, p, (p + k) % NP).wait_send()

        @pl.loop(1, LY)
        def _(k):
            l_copy(g, layer, (layer + k) % LY).wait_send()

        @pl.loop(1, LY * NP)
        def _(k):
            q = (mine + k) % (LY * NP)
            r_copy(g, q, mine, q).wait_send()


def shards(resid_stream, enc_mantissa, enc_exponent, enc_bias, dec_weight, dec_bias):
    width = resid_stream.shape[2]
    feats = enc_mantissa.shape[2]
    pairs, _, cols = dec_weight.shape
    blocks = width // BLK
    padded = (cols + BLK - 1) // BLK * BLK
    vm = pl.BlockSpec(memory_space=pltpu.VMEM)
    hbm = pl.BlockSpec(memory_space=pl.ANY)
    dma = pltpu.SemaphoreType.DMA
    bf, f32 = jnp.bfloat16, jnp.float32
    out = pl.pallas_call(
        kernel,
        out_shape=jax.ShapeDtypeStruct((1, width), bf),
        in_specs=[vm, hbm, vm, vm, hbm, vm],
        out_specs=vm,
        scratch_shapes=[
            pltpu.VMEM((width, feats), bf),
            pltpu.VMEM((pairs, cols, feats), bf),
            pltpu.VMEM((PITCH, BLK), f32),
            pltpu.VMEM((NZ, blocks, BLK), bf),
            pltpu.VMEM((GROUP * PITCH, BLK), f32),
            pltpu.VMEM((2, NP, GROUP, width), bf),
            pltpu.VMEM((LY, 2, NP * GROUP, feats), bf),
            pltpu.VMEM((2, LY, NP, GROUP, padded), bf),
            pltpu.VMEM((2, LY, NP, GROUP, padded), bf),
            pltpu.VMEM((GROUP * PITCH, BLK), f32),
            pltpu.VMEM((NZ, LY * padded // BLK, BLK), bf),
            pltpu.VMEM((NZ, LY * padded // BLK, BLK), bf),
            dma((2,)),
            dma((len(Z_STEPS),)), dma((len(PASSED),)), dma((NZ,)),
            dma((2, NP)), dma((2, NP)),
            dma((2, LY)), dma((2, LY)),
            dma((2, LY * NP)), dma((2, LY * NP)),
            dma((NZ,)), dma((NZ,)),
        ],
        compiler_params=pltpu.CompilerParams(collective_id=0, has_side_effects=True),
    )(
        resid_stream.reshape(1, width),
        enc_mantissa[0],
        enc_exponent.reshape(1, blocks),
        enc_bias,
        dec_weight.transpose(0, 2, 1),
        dec_bias,
    )
    return out[:, None, :]


def solution(mesh):
    in_specs = (
        P("feat", "layer", None),
        P("layer", None, "feat"),
        P("layer", None, "feat"),
        P("layer", "feat"),
        P(None, "feat", "layer"),
        P("layer", None),
    )
    out_specs = P("feat", "layer", None)
    return jax.shard_map(shards, mesh=mesh, in_specs=in_specs, out_specs=out_specs, check_vma=False)
```

```python
import jax
import jax.numpy as jnp
from jax import lax
from jax.experimental import pallas as pl
from jax.experimental.pallas import tpu as pltpu
from jax.sharding import PartitionSpec as P

LY = 4
NX = 4
NP = 8
NZ = 16
BLK = 128
PITCH = 24
MESH = pl.DeviceIdType.MESH
GROUP = 8
Z_STEPS = (8, 7, 9, 6, 10, 5, 11, 4, 12, 3, 13, 2, 14, 1, 15)
RING = (2, 1, 3, 0)
PLANE = sorted(
    ((dy, dx, dc) for dy in RING for dx in RING for dc in (1, 0) if dy or dx or dc),
    key=lambda s: -(min(s[0], 4 - s[0]) + min(s[1], 4 - s[1])),
)


def pow2(exponent):
    down = -exponent
    scale = jnp.ones(exponent.shape, jnp.float32)
    for bit in range(7):
        scale = scale * jnp.where((down & (1 << bit)) != 0, jnp.float32(2.0 ** -(1 << bit)), jnp.float32(1.0))
    return scale


def kernel(
    x_ref, m_ref, e_ref, eb_ref, d_ref, db_ref, out_ref,
    w_v, d_v, own, rows, stage, xg, lat, part, rs1, stage2, sb, rz,
    loc_sem, zs, zr, ps, pr, ls, lr, rs_s, rs_r, fs, fr,
):
    layer = lax.axis_index("layer")
    feat = lax.axis_index("feat")
    y_lo = feat // (NZ * NX)
    z = (feat // NX) % NZ
    x = feat % NX
    p = y_lo * NX + x
    y, core = layer // 2 * 2 + y_lo, layer % 2
    mine = layer * NP + p
    width = x_ref.shape[1]
    blocks = width // BLK
    cols = d_ref.shape[1]
    chunks = part.shape[4] // BLK

    def feat_of(place, zz):
        return (place // NX) * (NZ * NX) + zz * NX + place % NX

    def along(step):
        return (z + step + NZ) % NZ

    def plane_to(dy, dx, dc):
        to_y = (y + dy) % 4
        return (to_y // 2 * 2 + (core + dc) % 2) * NP + to_y % 2 * NX + (x + dx) % NX

    load_w = pltpu.make_async_copy(m_ref, w_v, loc_sem.at[0])
    load_d = pltpu.make_async_copy(d_ref, d_v, loc_sem.at[1])
    load_w.start()
    load_d.start()

    barrier = pltpu.get_barrier_semaphore()
    for step in Z_STEPS:
        pl.semaphore_signal(barrier, inc=1, device_id=(layer, feat_of(p, along(step))), device_id_type=MESH)
    for dy, dx, dc in PLANE:
        to = plane_to(dy, dx, dc)
        pl.semaphore_signal(barrier, inc=1, device_id=(to // NP, feat_of(to % NP, z)), device_id_type=MESH)

    for b in range(blocks):
        own[b : b + 1, :] = x_ref[0:1, b * BLK : (b + 1) * BLK].astype(jnp.float32)
    rows[z] = own[0:blocks, :].astype(jnp.bfloat16)
    for g in range(2):
        for t in range(LY):
            part[g, t, :, :, 512:640] = jnp.zeros((NP, GROUP, 128), jnp.bfloat16)

    pl.semaphore_wait(barrier, len(Z_STEPS) + len(PLANE))

    def z_copy(row, step):
        return pltpu.make_async_remote_copy(
            src_ref=rows.at[z], dst_ref=rows.at[row], send_sem=zs.at[along(step)], recv_sem=zr.at[row],
            device_id=(layer, feat_of(p, along(step))), device_id_type=MESH,
        )

    for step in Z_STEPS:
        z_copy(z, step).start()

    load_w.wait()
    scales = pow2(e_ref[0:1, :])
    for b in range(blocks):
        piece = slice(b * BLK, (b + 1) * BLK)
        w_v[piece, :] = (w_v[piece, :].astype(jnp.float32) * scales[0:1, b : b + 1]).astype(jnp.bfloat16)

    def p_copy(group, slot, other):
        return pltpu.make_async_remote_copy(
            src_ref=xg.at[group, p], dst_ref=xg.at[group, slot],
            send_sem=ps.at[group, other], recv_sem=pr.at[group, slot],
            device_id=(layer, feat_of(other, z)), device_id_type=MESH,
        )

    def spread(g):
        for i in range(GROUP):
            row = g * GROUP + i

            @pl.when(row != z)
            def _():
                z_copy(row, 1).wait_recv()

            stage[i * PITCH : i * PITCH + blocks, :] = rows[row].astype(jnp.float32)
        for b in range(blocks):
            xg[g, p, :, b * BLK : (b + 1) * BLK] = stage[pl.ds(b, GROUP, stride=PITCH), :].astype(jnp.bfloat16)
        for dy in (1, 0):
            for dx in RING:
                if dy or dx:
                    p_copy(g, p, (y_lo + dy) % 2 * NX + (x + dx) % NX).start()

    spread(0)
    spread(1)

    def l_copy(group, slot, other):
        return pltpu.make_async_remote_copy(
            src_ref=lat.at[layer, group], dst_ref=lat.at[slot, group],
            send_sem=ls.at[group, other], recv_sem=lr.at[group, slot],
            device_id=(other, feat), device_id_type=MESH,
        )

    tokens = NP * GROUP

    def encode(g):
        @pl.loop(1, NP)
        def _(k):
            other = (p + k) % NP
            p_copy(g, other, other).wait_recv()

        pre = jnp.dot(xg[g].reshape(tokens, width), w_v[...], preferred_element_type=jnp.float32)
        lat[layer, g] = jnp.maximum(pre + eb_ref[...], 0.0).astype(jnp.bfloat16)
        for k in (2, 3, 1):
            l_copy(g, layer, (layer + k) % LY).start()

    def r_copy(group, src, slot, other):
        return pltpu.make_async_remote_copy(
            src_ref=part.at[group, src // NP, src % NP], dst_ref=rs1.at[group, slot // NP, slot % NP],
            send_sem=rs_s.at[group, other], recv_sem=rs_r.at[group, slot],
            device_id=(other // NP, feat_of(other % NP, z)), device_id_type=MESH,
        )

    def decode(g):
        @pl.loop(1, LY)
        def _(k):
            other = (layer + k) % LY
            l_copy(g, other, other).wait_recv()

        for t in range(LY):
            total = jnp.zeros((tokens, cols), jnp.float32)
            for s in range(t + 1):
                total = total + lax.dot_general(
                    lat[s, g], d_v[t * (t + 1) // 2 + s], (((1,), (1,)), ((), ())),
                    preferred_element_type=jnp.float32,
                )
            part[g, t, :, :, 0:cols] = total.reshape(NP, GROUP, cols).astype(jnp.bfloat16)
        for dy, dx, dc in PLANE:
            to = plane_to(dy, dx, dc)
            r_copy(g, to, mine, to).start()
        rs1[g, layer, p] = part[g, layer, p]

    encode(0)
    encode(1)
    load_d.wait()
    decode(0)
    decode(1)

    def f_copy(row, slot):
        return pltpu.make_async_remote_copy(
            src_ref=sb.at[row], dst_ref=rz.at[slot], send_sem=fs.at[row], recv_sem=fr.at[slot],
            device_id=(layer, feat_of(p, row)), device_id_type=MESH,
        )

    def gathered(g):
        @pl.loop(1, LY * NP)
        def _(k):
            q = (mine + k) % (LY * NP)
            r_copy(g, q, q, q).wait_recv()

        for s in range(LY):
            total = rs1[g, s, 0].astype(jnp.float32)
            for place in range(1, NP):
                total = total + rs1[g, s, place].astype(jnp.float32)
            for c in range(chunks):
                stage2[pl.ds(s * chunks + c, GROUP, stride=PITCH), :] = total[:, c * BLK : (c + 1) * BLK]
        for i in range(GROUP):
            sb[g * GROUP + i] = stage2[i * PITCH : i * PITCH + LY * chunks, :].astype(jnp.bfloat16)

        for step in Z_STEPS:
            row = along(step)

            @pl.when(row // GROUP == g)
            def _():
                f_copy(row, z).start()

    gathered(0)
    gathered(1)
    rz[z] = sb[z]

    @pl.loop(1, NZ)
    def _(k):
        other = (z + k) % NZ
        f_copy(other, other).wait_recv()

    total = rz[0].astype(jnp.float32)
    for zz in range(1, NZ):
        total = total + rz[zz].astype(jnp.float32)

    half = BLK // 2
    low = lax.broadcasted_iota(jnp.int32, (1, BLK), 1) < half
    turned = pltpu.roll(total, half, 1)
    at = 0
    for pair in range(LY // 2):
        even, odd = pair * 2 * chunks, (pair * 2 + 1) * chunks
        pieces = [total[even + c : even + c + 1, :] for c in range(chunks - 1)]
        pieces.append(jnp.where(low, total[even + chunks - 1 : even + chunks, :], turned[odd : odd + 1, :]))
        for c in range(1, chunks):
            pieces.append(jnp.where(low, turned[odd + c - 1 : odd + c, :], turned[odd + c : odd + c + 1, :]))
        for piece in pieces:
            out_ref[0:1, at : at + BLK] = (piece + db_ref[0:1, at : at + BLK]).astype(jnp.bfloat16)
            at += BLK

    @pl.loop(1, NZ)
    def _(k):
        z_copy(z, k).wait_send()
        f_copy((z + k) % NZ, z).wait_send()

    for g in range(2):
        @pl.loop(1, NP)
        def _(k):
            p_copy(g, p, (p + k) % NP).wait_send()

        @pl.loop(1, LY)
        def _(k):
            l_copy(g, layer, (layer + k) % LY).wait_send()

        @pl.loop(1, LY * NP)
        def _(k):
            q = (mine + k) % (LY * NP)
            r_copy(g, q, mine, q).wait_send()


def shards(resid_stream, enc_mantissa, enc_exponent, enc_bias, dec_weight, dec_bias):
    width = resid_stream.shape[2]
    feats = enc_mantissa.shape[2]
    pairs, _, cols = dec_weight.shape
    blocks = width // BLK
    padded = (cols + BLK - 1) // BLK * BLK
    vm = pl.BlockSpec(memory_space=pltpu.VMEM)
    hbm = pl.BlockSpec(memory_space=pl.ANY)
    dma = pltpu.SemaphoreType.DMA
    bf, f32 = jnp.bfloat16, jnp.float32
    out = pl.pallas_call(
        kernel,
        out_shape=jax.ShapeDtypeStruct((1, width), bf),
        in_specs=[vm, hbm, vm, vm, hbm, vm],
        out_specs=vm,
        scratch_shapes=[
            pltpu.VMEM((width, feats), bf),
            pltpu.VMEM((pairs, cols, feats), bf),
            pltpu.VMEM((PITCH, BLK), f32),
            pltpu.VMEM((NZ, blocks, BLK), bf),
            pltpu.VMEM((GROUP * PITCH, BLK), f32),
            pltpu.VMEM((2, NP, GROUP, width), bf),
            pltpu.VMEM((LY, 2, NP * GROUP, feats), bf),
            pltpu.VMEM((2, LY, NP, GROUP, padded), bf),
            pltpu.VMEM((2, LY, NP, GROUP, padded), bf),
            pltpu.VMEM((GROUP * PITCH, BLK), f32),
            pltpu.VMEM((NZ, LY * padded // BLK, BLK), bf),
            pltpu.VMEM((NZ, LY * padded // BLK, BLK), bf),
            dma((2,)),
            dma((NZ,)), dma((NZ,)),
            dma((2, NP)), dma((2, NP)),
            dma((2, LY)), dma((2, LY)),
            dma((2, LY * NP)), dma((2, LY * NP)),
            dma((NZ,)), dma((NZ,)),
        ],
        compiler_params=pltpu.CompilerParams(collective_id=0, has_side_effects=True),
    )(
        resid_stream.reshape(1, width),
        enc_mantissa[0],
        enc_exponent.reshape(1, blocks),
        enc_bias,
        dec_weight.transpose(0, 2, 1),
        dec_bias,
    )
    return out[:, None, :]


def solution(mesh):
    in_specs = (
        P("feat", "layer", None),
        P("layer", None, "feat"),
        P("layer", None, "feat"),
        P("layer", "feat"),
        P(None, "feat", "layer"),
        P("layer", None),
    )
    out_specs = P("feat", "layer", None)
    return jax.shard_map(shards, mesh=mesh, in_specs=in_specs, out_specs=out_specs, check_vma=False)
```

```python
import jax
import jax.numpy as jnp
from jax import lax
from jax.experimental import pallas as pl
from jax.experimental.pallas import tpu as pltpu
from jax.sharding import PartitionSpec as P

LY = 4
NX = 4
NP = 8
NZ = 16
BLK = 128
PITCH = 24
MESH = pl.DeviceIdType.MESH
SIZES = (4, 4, 8)
STARTS = tuple(sum(SIZES[:n]) for n in range(len(SIZES)))
GROUPS = range(len(SIZES))
Z_STEPS = (8, 7, 9, 6, 10, 5, 11, 4, 12, 3, 13, 2, 14, 1, 15)
RING = (2, 1, 3, 0)
CROSS = [(2, 0, 0), (0, 2, 0), (1, 0, 0), (3, 0, 0), (0, 1, 0), (0, 3, 0), (0, 0, 1)]
PLANE = sorted(
    ((dy, dx, dc) for dy in RING for dx in RING for dc in (1, 0) if dy or dx or dc),
    key=lambda s: -(min(s[0], 4 - s[0]) + min(s[1], 4 - s[1])),
)


def pow2(exponent):
    down = -exponent
    scale = jnp.ones(exponent.shape, jnp.float32)
    for bit in range(7):
        scale = scale * jnp.where((down & (1 << bit)) != 0, jnp.float32(2.0 ** -(1 << bit)), jnp.float32(1.0))
    return scale


def kernel(
    x_in, m_ref, e_in, eb_in, d_ref, db_in, out_ref,
    x_ref, e_ref, eb_ref, db_ref, w_v, d_v, own, rows, stage, xgs, lat, parts, rs1s, stage2, sb, rz,
    loc_sem, ready, zs, zr, ps, pr, ls, lr, rs_s, rs_r, fs, fr,
):
    layer = lax.axis_index("layer")
    feat = lax.axis_index("feat")
    y_lo = feat // (NZ * NX)
    z = (feat // NX) % NZ
    x = feat % NX
    p = y_lo * NX + x
    y, core = layer // 2 * 2 + y_lo, layer % 2
    mine = layer * NP + p
    width = x_in.shape[1]
    blocks = width // BLK
    cols = d_ref.shape[1]
    chunks = parts[0].shape[3] // BLK

    def feat_of(place, zz):
        return (place // NX) * (NZ * NX) + zz * NX + place % NX

    def rows_of(group):
        return slice(STARTS[group] * NP, (STARTS[group] + SIZES[group]) * NP)

    def along(step):
        return (z + step + NZ) % NZ

    def plane_to(dy, dx, dc):
        to_y = (y + dy) % 4
        return (to_y // 2 * 2 + (core + dc) % 2) * NP + to_y % 2 * NX + (x + dx) % NX

    small = [
        pltpu.make_async_copy(src, dst, loc_sem.at[2 + n])
        for n, (src, dst) in enumerate(((x_in, x_ref), (e_in, e_ref), (eb_in, eb_ref), (db_in, db_ref)))
    ]
    load_w = pltpu.make_async_copy(m_ref, w_v, loc_sem.at[0])
    load_d = pltpu.make_async_copy(d_ref, d_v, loc_sem.at[1])

    barrier = pltpu.get_barrier_semaphore()
    for step in Z_STEPS:
        pl.semaphore_signal(barrier, inc=1, device_id=(layer, feat_of(p, along(step))), device_id_type=MESH)
    for dy, dx, dc in CROSS:
        to = plane_to(dy, dx, dc)
        pl.semaphore_signal(barrier, inc=1, device_id=(to // NP, feat_of(to % NP, z)), device_id_type=MESH)
    for copy in small:
        copy.start()
    load_w.start()
    load_d.start()
    small[0].wait()

    for b in range(blocks):
        own[b : b + 1, :] = x_ref[0:1, b * BLK : (b + 1) * BLK].astype(jnp.float32)
    rows[z] = own[0:blocks, :].astype(jnp.bfloat16)
    for g in GROUPS:
        for t in range(LY):
            parts[g][t, :, :, 512:640] = jnp.zeros((NP, SIZES[g], 128), jnp.bfloat16)

    pl.semaphore_wait(barrier, len(Z_STEPS) + len(CROSS))

    def z_copy(row, step):
        return pltpu.make_async_remote_copy(
            src_ref=rows.at[z], dst_ref=rows.at[row], send_sem=zs.at[along(step)], recv_sem=zr.at[row],
            device_id=(layer, feat_of(p, along(step))), device_id_type=MESH,
        )

    for step in Z_STEPS:
        z_copy(z, step).start()

    for dx in RING[:3]:
        to = plane_to(0, dx, 0)
        pl.semaphore_signal(ready.at[0], inc=1, device_id=(to // NP, feat_of(to % NP, z)), device_id_type=MESH)

    for copy in small[1:]:
        copy.wait()
    load_w.wait()
    scales = pow2(e_ref[0:1, :])
    for b in range(blocks):
        piece = slice(b * BLK, (b + 1) * BLK)
        w_v[piece, :] = (w_v[piece, :].astype(jnp.float32) * scales[0:1, b : b + 1]).astype(jnp.bfloat16)

    pl.semaphore_wait(ready.at[0], NX - 1)
    to = plane_to(0, 0, 1)
    pl.semaphore_signal(ready.at[1], inc=1, device_id=(to // NP, feat), device_id_type=MESH)

    def p_copy(group, slot, other):
        return pltpu.make_async_remote_copy(
            src_ref=xgs[group].at[p], dst_ref=xgs[group].at[slot],
            send_sem=ps.at[group, other], recv_sem=pr.at[group, slot],
            device_id=(layer, feat_of(other, z)), device_id_type=MESH,
        )

    def spread(g):
        for i in range(SIZES[g]):
            row = STARTS[g] + i

            @pl.when(row != z)
            def _():
                z_copy(row, 1).wait_recv()

            stage[i * PITCH : i * PITCH + blocks, :] = rows[row].astype(jnp.float32)
        for b in range(blocks):
            xgs[g][p, :, b * BLK : (b + 1) * BLK] = stage[pl.ds(b, SIZES[g], stride=PITCH), :].astype(jnp.bfloat16)
        for dy in (1, 0):
            for dx in RING:
                if dy or dx:
                    p_copy(g, p, (y_lo + dy) % 2 * NX + (x + dx) % NX).start()

    for g in GROUPS:
        spread(g)

    def l_copy(group, slot, other):
        return pltpu.make_async_remote_copy(
            src_ref=lat.at[layer, rows_of(group)], dst_ref=lat.at[slot, rows_of(group)],
            send_sem=ls.at[group, other], recv_sem=lr.at[group, slot],
            device_id=(other, feat), device_id_type=MESH,
        )


    def encode(g):
        @pl.loop(1, NP)
        def _(k):
            other = (p + k) % NP
            p_copy(g, other, other).wait_recv()

        pre = jnp.dot(xgs[g][...].reshape(NP * SIZES[g], width), w_v[...], preferred_element_type=jnp.float32)
        lat[layer, rows_of(g)] = jnp.maximum(pre + eb_ref[...], 0.0).astype(jnp.bfloat16)
        for k in (2, 3, 1):
            l_copy(g, layer, (layer + k) % LY).start()

    def r_copy(group, src, slot, other):
        return pltpu.make_async_remote_copy(
            src_ref=parts[group].at[src // NP, src % NP], dst_ref=rs1s[group].at[slot // NP, slot % NP],
            send_sem=rs_s.at[group, other], recv_sem=rs_r.at[group, slot],
            device_id=(other // NP, feat_of(other % NP, z)), device_id_type=MESH,
        )

    def decode(g):
        @pl.loop(1, LY)
        def _(k):
            other = (layer + k) % LY
            l_copy(g, other, other).wait_recv()

        for t in range(LY):
            total = jnp.zeros((NP * SIZES[g], cols), jnp.float32)
            for s in range(t + 1):
                total = total + lax.dot_general(
                    lat[s, rows_of(g)], d_v[t * (t + 1) // 2 + s], (((1,), (1,)), ((), ())),
                    preferred_element_type=jnp.float32,
                )
            parts[g][t, :, :, 0:cols] = total.reshape(NP, SIZES[g], cols).astype(jnp.bfloat16)
        for dy, dx, dc in PLANE:
            to = plane_to(dy, dx, dc)
            r_copy(g, to, mine, to).start()
        rs1s[g][layer, p] = parts[g][layer, p]

    pl.semaphore_wait(ready.at[1], 1)
    for g in GROUPS:
        encode(g)
    load_d.wait()
    for g in GROUPS:
        decode(g)

    def f_copy(row, slot):
        return pltpu.make_async_remote_copy(
            src_ref=sb.at[row], dst_ref=rz.at[slot], send_sem=fs.at[row], recv_sem=fr.at[slot],
            device_id=(layer, feat_of(p, row)), device_id_type=MESH,
        )

    def gathered(g):
        @pl.loop(1, LY * NP)
        def _(k):
            q = (mine + k) % (LY * NP)
            r_copy(g, q, q, q).wait_recv()

        for s in range(LY):
            total = rs1s[g][s, 0].astype(jnp.float32)
            for place in range(1, NP):
                total = total + rs1s[g][s, place].astype(jnp.float32)
            for c in range(chunks):
                stage2[pl.ds(s * chunks + c, SIZES[g], stride=PITCH), :] = total[:, c * BLK : (c + 1) * BLK]
        for i in range(SIZES[g]):
            sb[STARTS[g] + i] = stage2[i * PITCH : i * PITCH + LY * chunks, :].astype(jnp.bfloat16)

        for step in Z_STEPS:
            row = along(step)

            @pl.when((row >= STARTS[g]) & (row < STARTS[g] + SIZES[g]))
            def _():
                f_copy(row, z).start()

    for g in GROUPS:
        gathered(g)
    rz[z] = sb[z]

    @pl.loop(1, NZ)
    def _(k):
        other = (z + k) % NZ
        f_copy(other, other).wait_recv()

    total = rz[0].astype(jnp.float32)
    for zz in range(1, NZ):
        total = total + rz[zz].astype(jnp.float32)

    half = BLK // 2
    low = lax.broadcasted_iota(jnp.int32, (1, BLK), 1) < half
    turned = pltpu.roll(total, half, 1)
    at = 0
    for pair in range(LY // 2):
        even, odd = pair * 2 * chunks, (pair * 2 + 1) * chunks
        pieces = [total[even + c : even + c + 1, :] for c in range(chunks - 1)]
        pieces.append(jnp.where(low, total[even + chunks - 1 : even + chunks, :], turned[odd : odd + 1, :]))
        for c in range(1, chunks):
            pieces.append(jnp.where(low, turned[odd + c - 1 : odd + c, :], turned[odd + c : odd + c + 1, :]))
        for piece in pieces:
            out_ref[0:1, at : at + BLK] = (piece + db_ref[0:1, at : at + BLK]).astype(jnp.bfloat16)
            at += BLK

    @pl.loop(1, NZ)
    def _(k):
        z_copy(z, k).wait_send()
        f_copy((z + k) % NZ, z).wait_send()

    for g in GROUPS:
        @pl.loop(1, NP)
        def _(k):
            p_copy(g, p, (p + k) % NP).wait_send()

        @pl.loop(1, LY)
        def _(k):
            l_copy(g, layer, (layer + k) % LY).wait_send()

        @pl.loop(1, LY * NP)
        def _(k):
            q = (mine + k) % (LY * NP)
            r_copy(g, q, mine, q).wait_send()


def shards(resid_stream, enc_mantissa, enc_exponent, enc_bias, dec_weight, dec_bias):
    width = resid_stream.shape[2]
    feats = enc_mantissa.shape[2]
    pairs, _, cols = dec_weight.shape
    blocks = width // BLK
    padded = (cols + BLK - 1) // BLK * BLK
    vm = pl.BlockSpec(memory_space=pltpu.VMEM)
    hbm = pl.BlockSpec(memory_space=pl.ANY)
    dma = pltpu.SemaphoreType.DMA
    bf, f32 = jnp.bfloat16, jnp.float32
    out = pl.pallas_call(
        kernel,
        out_shape=jax.ShapeDtypeStruct((1, width), bf),
        in_specs=[hbm] * 6,
        out_specs=vm,
        scratch_shapes=[
            pltpu.VMEM((1, width), bf),
            pltpu.VMEM((1, blocks), jnp.int32),
            pltpu.VMEM((1, feats), f32),
            pltpu.VMEM((1, width), f32),
            pltpu.VMEM((width, feats), bf),
            pltpu.VMEM((pairs, cols, feats), bf),
            pltpu.VMEM((PITCH, BLK), f32),
            pltpu.VMEM((NZ, blocks, BLK), bf),
            pltpu.VMEM((max(SIZES) * PITCH, BLK), f32),
            [pltpu.VMEM((NP, size, width), bf) for size in SIZES],
            pltpu.VMEM((LY, NP * NZ, feats), bf),
            [pltpu.VMEM((LY, NP, size, padded), bf) for size in SIZES],
            [pltpu.VMEM((LY, NP, size, padded), bf) for size in SIZES],
            pltpu.VMEM((max(SIZES) * PITCH, BLK), f32),
            pltpu.VMEM((NZ, LY * padded // BLK, BLK), bf),
            pltpu.VMEM((NZ, LY * padded // BLK, BLK), bf),
            dma((6,)),
            pltpu.SemaphoreType.REGULAR((2,)),
            dma((NZ,)), dma((NZ,)),
            dma((len(SIZES), NP)), dma((len(SIZES), NP)),
            dma((len(SIZES), LY)), dma((len(SIZES), LY)),
            dma((len(SIZES), LY * NP)), dma((len(SIZES), LY * NP)),
            dma((NZ,)), dma((NZ,)),
        ],
        compiler_params=pltpu.CompilerParams(collective_id=0, has_side_effects=True),
    )(
        resid_stream.reshape(1, width),
        enc_mantissa[0],
        enc_exponent.reshape(1, blocks),
        enc_bias,
        dec_weight.transpose(0, 2, 1),
        dec_bias,
    )
    return out[:, None, :]


def solution(mesh):
    in_specs = (
        P("feat", "layer", None),
        P("layer", None, "feat"),
        P("layer", None, "feat"),
        P("layer", "feat"),
        P(None, "feat", "layer"),
        P("layer", None),
    )
    out_specs = P("feat", "layer", None)
    return jax.shard_map(shards, mesh=mesh, in_specs=in_specs, out_specs=out_specs, check_vma=False)
```

```python
import jax
import jax.numpy as jnp
from jax import lax
from jax.experimental import pallas as pl
from jax.experimental.pallas import tpu as pltpu
from jax.sharding import PartitionSpec as P

LY = 4
NX = 4
NP = 8
NZ = 16
BLK = 128
PITCH = 24
MESH = pl.DeviceIdType.MESH
SIZES = (4, 4, 8)
STARTS = tuple(sum(SIZES[:n]) for n in range(len(SIZES)))
GROUPS = range(len(SIZES))
Z_STEPS = (8, 7, 9, 6, 10, 5, 11, 4, 12, 3, 13, 2, 14, 1, 15)
RING = (2, 1, 3, 0)
CROSS = [(2, 0, 0), (0, 2, 0), (1, 0, 0), (3, 0, 0), (0, 1, 0), (0, 3, 0), (0, 0, 1)]
PLANE = sorted(
    ((dy, dx, dc) for dy in RING for dx in RING for dc in (1, 0) if dy or dx or dc),
    key=lambda s: -(min(s[0], 4 - s[0]) + min(s[1], 4 - s[1])),
)


def pow2(exponent):
    down = -exponent
    scale = jnp.ones(exponent.shape, jnp.float32)
    for bit in range(7):
        scale = scale * jnp.where((down & (1 << bit)) != 0, jnp.float32(2.0 ** -(1 << bit)), jnp.float32(1.0))
    return scale


def kernel(
    x_in, m_ref, e_in, eb_in, d_ref, db_in, out_ref,
    x_ref, e_ref, eb_ref, db_ref, w_v, d_v, own, rows, stage, xgs, lat, parts, rs1s, stage2, sb, rz,
    loc_sem, ready, zs, zr, ps, pr, ls, lr, rs_s, rs_r, fs, fr,
):
    layer = lax.axis_index("layer")
    feat = lax.axis_index("feat")
    y_hi = jnp.where(layer >= 2, 1, 0)
    core = layer - 2 * y_hi
    y_lo = jnp.where(feat >= NZ * NX, 1, 0)
    z = lax.div(feat - y_lo * (NZ * NX), NX)
    x = feat - y_lo * (NZ * NX) - z * NX
    p = y_lo * NX + x
    y = 2 * y_hi + y_lo
    width = x_in.shape[1]
    blocks = width // BLK
    cols = d_ref.shape[1]
    chunks = parts[0].shape[3] // BLK

    def feat_of(place, zz):
        return place + jnp.where(place >= NX, NZ * NX - NX, 0) + zz * NX

    def wrap(value, length):
        return jnp.where(value >= length, value - length, value)

    def rows_of(group):
        return slice(STARTS[group] * NP, (STARTS[group] + SIZES[group]) * NP)

    def along(step):
        return wrap(z + step, NZ)

    def plane_to(dy, dx, dc):
        to_y = wrap(y + dy, 4)
        to_core = 1 - core if dc else core
        to_lo = 1 - y_lo if dy % 2 else y_lo
        return jnp.where(to_y >= 2, 2, 0) + to_core, to_lo * NX + wrap(x + dx, NX)

    small = [
        pltpu.make_async_copy(src, dst, loc_sem.at[2 + n])
        for n, (src, dst) in enumerate(((x_in, x_ref), (e_in, e_ref), (eb_in, eb_ref), (db_in, db_ref)))
    ]
    load_w = pltpu.make_async_copy(m_ref, w_v, loc_sem.at[0])
    load_d = pltpu.make_async_copy(d_ref, d_v, loc_sem.at[1])

    barrier = pltpu.get_barrier_semaphore()
    for step in Z_STEPS:
        pl.semaphore_signal(barrier, inc=1, device_id=(layer, feat_of(p, along(step))), device_id_type=MESH)
    for dy, dx, dc in CROSS:
        to = plane_to(dy, dx, dc)
        pl.semaphore_signal(barrier, inc=1, device_id=(to[0], feat_of(to[1], z)), device_id_type=MESH)
    for copy in small:
        copy.start()
    load_w.start()
    load_d.start()
    small[0].wait()

    for b in range(blocks):
        own[b : b + 1, :] = x_ref[0:1, b * BLK : (b + 1) * BLK].astype(jnp.float32)
    rows[z] = own[0:blocks, :].astype(jnp.bfloat16)
    for g in GROUPS:
        for t in range(LY):
            parts[g][t, :, :, 512:640] = jnp.zeros((NP, SIZES[g], 128), jnp.bfloat16)

    pl.semaphore_wait(barrier, len(Z_STEPS) + len(CROSS))

    def z_copy(row, step):
        return pltpu.make_async_remote_copy(
            src_ref=rows.at[z], dst_ref=rows.at[row], send_sem=zs.at[along(step)], recv_sem=zr.at[row],
            device_id=(layer, feat_of(p, along(step))), device_id_type=MESH,
        )

    for step in Z_STEPS:
        z_copy(z, step).start()

    for dx in RING[:3]:
        to = plane_to(0, dx, 0)
        pl.semaphore_signal(ready.at[0], inc=1, device_id=(to[0], feat_of(to[1], z)), device_id_type=MESH)

    for copy in small[1:]:
        copy.wait()
    load_w.wait()
    scales = pow2(e_ref[0:1, :])
    for b in range(blocks):
        piece = slice(b * BLK, (b + 1) * BLK)
        w_v[piece, :] = (w_v[piece, :].astype(jnp.float32) * scales[0:1, b : b + 1]).astype(jnp.bfloat16)

    pl.semaphore_wait(ready.at[0], NX - 1)
    to = plane_to(0, 0, 1)
    pl.semaphore_signal(ready.at[1], inc=1, device_id=(to[0], feat), device_id_type=MESH)

    def p_copy(group, slot, other):
        return pltpu.make_async_remote_copy(
            src_ref=xgs[group].at[p], dst_ref=xgs[group].at[slot],
            send_sem=ps.at[group, other], recv_sem=pr.at[group, slot],
            device_id=(layer, feat_of(other, z)), device_id_type=MESH,
        )

    def spread(g):
        for i in range(SIZES[g]):
            row = STARTS[g] + i

            @pl.when(row != z)
            def _():
                z_copy(row, 1).wait_recv()

            stage[i * PITCH : i * PITCH + blocks, :] = rows[row].astype(jnp.float32)
        for b in range(blocks):
            xgs[g][p, :, b * BLK : (b + 1) * BLK] = stage[pl.ds(b, SIZES[g], stride=PITCH), :].astype(jnp.bfloat16)
        for dy in (1, 0):
            for dx in RING:
                if dy or dx:
                    p_copy(g, p, plane_to(dy, dx, 0)[1]).start()

    for g in GROUPS:
        spread(g)

    def l_copy(group, slot, other):
        return pltpu.make_async_remote_copy(
            src_ref=lat.at[layer, rows_of(group)], dst_ref=lat.at[slot, rows_of(group)],
            send_sem=ls.at[group, other], recv_sem=lr.at[group, slot],
            device_id=(other, feat), device_id_type=MESH,
        )


    def encode(g):
        @pl.loop(1, NP)
        def _(k):
            other = wrap(p + k, NP)
            p_copy(g, other, other).wait_recv()

        pre = jnp.dot(xgs[g][...].reshape(NP * SIZES[g], width), w_v[...], preferred_element_type=jnp.float32)
        lat[layer, rows_of(g)] = jnp.maximum(pre + eb_ref[...], 0.0).astype(jnp.bfloat16)
        for k in (2, 3, 1):
            l_copy(g, layer, wrap(layer + k, LY)).start()

    def r_copy(group, n):
        to = plane_to(*PLANE[n])
        return pltpu.make_async_remote_copy(
            src_ref=parts[group].at[to[0], to[1]], dst_ref=rs1s[group].at[layer, p],
            send_sem=rs_s.at[group, n], recv_sem=rs_r.at[group, n],
            device_id=(to[0], feat_of(to[1], z)), device_id_type=MESH,
        )

    def decode(g):
        @pl.loop(1, LY)
        def _(k):
            other = wrap(layer + k, LY)
            l_copy(g, other, other).wait_recv()

        for t in range(LY):
            total = jnp.zeros((NP * SIZES[g], cols), jnp.float32)
            for s in range(t + 1):
                total = total + lax.dot_general(
                    lat[s, rows_of(g)], d_v[t * (t + 1) // 2 + s], (((1,), (1,)), ((), ())),
                    preferred_element_type=jnp.float32,
                )
            parts[g][t, :, :, 0:cols] = total.reshape(NP, SIZES[g], cols).astype(jnp.bfloat16)
        for n in range(len(PLANE)):
            r_copy(g, n).start()
        rs1s[g][layer, p] = parts[g][layer, p]

    pl.semaphore_wait(ready.at[1], 1)
    for g in GROUPS:
        encode(g)
    load_d.wait()
    for g in GROUPS:
        decode(g)

    def f_copy(row, slot):
        return pltpu.make_async_remote_copy(
            src_ref=sb.at[row], dst_ref=rz.at[slot], send_sem=fs.at[row], recv_sem=fr.at[slot],
            device_id=(layer, feat_of(p, row)), device_id_type=MESH,
        )

    def gathered(g):
        for n in range(len(PLANE)):
            r_copy(g, n).wait_recv()

        for s in range(LY):
            total = rs1s[g][s, 0].astype(jnp.float32)
            for place in range(1, NP):
                total = total + rs1s[g][s, place].astype(jnp.float32)
            for c in range(chunks):
                stage2[pl.ds(s * chunks + c, SIZES[g], stride=PITCH), :] = total[:, c * BLK : (c + 1) * BLK]
        for i in range(SIZES[g]):
            sb[STARTS[g] + i] = stage2[i * PITCH : i * PITCH + LY * chunks, :].astype(jnp.bfloat16)

        for step in Z_STEPS:
            row = along(step)

            @pl.when((row >= STARTS[g]) & (row < STARTS[g] + SIZES[g]))
            def _():
                f_copy(row, z).start()

    for g in GROUPS:
        gathered(g)
    rz[z] = sb[z]

    @pl.loop(1, NZ)
    def _(k):
        other = wrap(z + k, NZ)
        f_copy(other, other).wait_recv()

    total = rz[0].astype(jnp.float32)
    for zz in range(1, NZ):
        total = total + rz[zz].astype(jnp.float32)

    half = BLK // 2
    low = lax.broadcasted_iota(jnp.int32, (1, BLK), 1) < half
    turned = pltpu.roll(total, half, 1)
    at = 0
    for pair in range(LY // 2):
        even, odd = pair * 2 * chunks, (pair * 2 + 1) * chunks
        pieces = [total[even + c : even + c + 1, :] for c in range(chunks - 1)]
        pieces.append(jnp.where(low, total[even + chunks - 1 : even + chunks, :], turned[odd : odd + 1, :]))
        for c in range(1, chunks):
            pieces.append(jnp.where(low, turned[odd + c - 1 : odd + c, :], turned[odd + c : odd + c + 1, :]))
        for piece in pieces:
            out_ref[0:1, at : at + BLK] = (piece + db_ref[0:1, at : at + BLK]).astype(jnp.bfloat16)
            at += BLK

    @pl.loop(1, NZ)
    def _(k):
        z_copy(z, k).wait_send()
        f_copy(wrap(z + k, NZ), z).wait_send()

    for g in GROUPS:
        @pl.loop(1, NP)
        def _(k):
            p_copy(g, p, wrap(p + k, NP)).wait_send()

        @pl.loop(1, LY)
        def _(k):
            l_copy(g, layer, wrap(layer + k, LY)).wait_send()

        for n in range(len(PLANE)):
            r_copy(g, n).wait_send()


def shards(resid_stream, enc_mantissa, enc_exponent, enc_bias, dec_weight, dec_bias):
    width = resid_stream.shape[2]
    feats = enc_mantissa.shape[2]
    pairs, _, cols = dec_weight.shape
    blocks = width // BLK
    padded = (cols + BLK - 1) // BLK * BLK
    vm = pl.BlockSpec(memory_space=pltpu.VMEM)
    hbm = pl.BlockSpec(memory_space=pl.ANY)
    dma = pltpu.SemaphoreType.DMA
    bf, f32 = jnp.bfloat16, jnp.float32
    out = pl.pallas_call(
        kernel,
        out_shape=jax.ShapeDtypeStruct((1, width), bf),
        in_specs=[hbm] * 6,
        out_specs=vm,
        scratch_shapes=[
            pltpu.VMEM((1, width), bf),
            pltpu.VMEM((1, blocks), jnp.int32),
            pltpu.VMEM((1, feats), f32),
            pltpu.VMEM((1, width), f32),
            pltpu.VMEM((width, feats), bf),
            pltpu.VMEM((pairs, cols, feats), bf),
            pltpu.VMEM((PITCH, BLK), f32),
            pltpu.VMEM((NZ, blocks, BLK), bf),
            pltpu.VMEM((max(SIZES) * PITCH, BLK), f32),
            [pltpu.VMEM((NP, size, width), bf) for size in SIZES],
            pltpu.VMEM((LY, NP * NZ, feats), bf),
            [pltpu.VMEM((LY, NP, size, padded), bf) for size in SIZES],
            [pltpu.VMEM((LY, NP, size, padded), bf) for size in SIZES],
            pltpu.VMEM((max(SIZES) * PITCH, BLK), f32),
            pltpu.VMEM((NZ, LY * padded // BLK, BLK), bf),
            pltpu.VMEM((NZ, LY * padded // BLK, BLK), bf),
            dma((6,)),
            pltpu.SemaphoreType.REGULAR((2,)),
            dma((NZ,)), dma((NZ,)),
            dma((len(SIZES), NP)), dma((len(SIZES), NP)),
            dma((len(SIZES), LY)), dma((len(SIZES), LY)),
            dma((len(SIZES), LY * NP)), dma((len(SIZES), LY * NP)),
            dma((NZ,)), dma((NZ,)),
        ],
        compiler_params=pltpu.CompilerParams(collective_id=0, has_side_effects=True),
    )(
        resid_stream.reshape(1, width),
        enc_mantissa[0],
        enc_exponent.reshape(1, blocks),
        enc_bias,
        dec_weight.transpose(0, 2, 1),
        dec_bias,
    )
    return out[:, None, :]


def solution(mesh):
    in_specs = (
        P("feat", "layer", None),
        P("layer", None, "feat"),
        P("layer", None, "feat"),
        P("layer", "feat"),
        P(None, "feat", "layer"),
        P("layer", None),
    )
    out_specs = P("feat", "layer", None)
    return jax.shard_map(shards, mesh=mesh, in_specs=in_specs, out_specs=out_specs, check_vma=False)
```

```python
import jax
import jax.numpy as jnp
from jax import lax
from jax.experimental import pallas as pl
from jax.experimental.pallas import tpu as pltpu
from jax.sharding import PartitionSpec as P

LY = 4
NX = 4
NP = 8
NZ = 16
BLK = 128
PITCH = 24
MESH = pl.DeviceIdType.MESH
SIZES = (4, 4, 8)
STARTS = tuple(sum(SIZES[:n]) for n in range(len(SIZES)))
GROUPS = range(len(SIZES))
Z_STEPS = (8, 7, 9, 6, 10, 5, 11, 4, 12, 3, 13, 2, 14, 1, 15)
RING = (2, 1, 3, 0)
CROSS = [(2, 0, 0), (0, 2, 0), (1, 0, 0), (3, 0, 0), (0, 1, 0), (0, 3, 0), (0, 0, 1)]
PLANE = sorted(
    ((dy, dx, dc) for dy in RING for dx in RING for dc in (1, 0) if dy or dx or dc),
    key=lambda s: -(min(s[0], 4 - s[0]) + min(s[1], 4 - s[1])),
)


def pow2(exponent):
    down = -exponent
    scale = jnp.ones(exponent.shape, jnp.float32)
    for bit in range(7):
        scale = scale * jnp.where((down & (1 << bit)) != 0, jnp.float32(2.0 ** -(1 << bit)), jnp.float32(1.0))
    return scale


def kernel(
    x_in, m_ref, e_in, eb_in, d_ref, db_in, out_ref,
    x_ref, e_ref, eb_ref, db_ref, w_v, d_v, own, rows, stage, xgs, lat, parts, rs1s, stage2, sb, rz,
    loc_sem, ready, zs, zr, ps, pr, ls, lr, rs_s, rs_r, fs, fr,
):
    layer = lax.axis_index("layer")
    feat = lax.axis_index("feat")
    y_hi = jnp.where(layer >= 2, 1, 0)
    core = layer - 2 * y_hi
    y_lo = jnp.where(feat >= NZ * NX, 1, 0)
    z = lax.div(feat - y_lo * (NZ * NX), NX)
    x = feat - y_lo * (NZ * NX) - z * NX
    p = y_lo * NX + x
    y = 2 * y_hi + y_lo
    width = x_in.shape[1]
    blocks = width // BLK
    cols = d_ref.shape[1]
    chunks = parts[0].shape[3] // BLK

    def feat_of(place, zz):
        return place + jnp.where(place >= NX, NZ * NX - NX, 0) + zz * NX

    def wrap(value, length):
        return jnp.where(value >= length, value - length, value)

    def rows_of(group):
        return slice(STARTS[group] * NP, (STARTS[group] + SIZES[group]) * NP)

    def along(step):
        return wrap(z + step, NZ)

    def plane_to(dy, dx, dc):
        to_y = wrap(y + dy, 4)
        to_core = 1 - core if dc else core
        to_lo = 1 - y_lo if dy % 2 else y_lo
        return jnp.where(to_y >= 2, 2, 0) + to_core, to_lo * NX + wrap(x + dx, NX)

    small = [
        pltpu.make_async_copy(src, dst, loc_sem.at[2 + n])
        for n, (src, dst) in enumerate(((x_in, x_ref), (e_in, e_ref), (eb_in, eb_ref), (db_in, db_ref)))
    ]
    load_w = pltpu.make_async_copy(m_ref, w_v, loc_sem.at[0])
    load_d = pltpu.make_async_copy(d_ref, d_v, loc_sem.at[1])

    barrier = pltpu.get_barrier_semaphore()
    for step in Z_STEPS:
        pl.semaphore_signal(barrier, inc=1, device_id=(layer, feat_of(p, along(step))), device_id_type=MESH)
    for dy, dx, dc in CROSS:
        to = plane_to(dy, dx, dc)
        pl.semaphore_signal(barrier, inc=1, device_id=(to[0], feat_of(to[1], z)), device_id_type=MESH)
    for copy in small:
        copy.start()
    load_w.start()
    load_d.start()
    small[0].wait()

    for b in range(blocks):
        own[b : b + 1, :] = x_ref[0:1, b * BLK : (b + 1) * BLK].astype(jnp.float32)
    rows[z] = own[0:blocks, :].astype(jnp.bfloat16)
    for g in GROUPS:
        for t in range(LY):
            parts[g][t, :, :, 512:640] = jnp.zeros((NP, SIZES[g], 128), jnp.bfloat16)

    pl.semaphore_wait(barrier, len(Z_STEPS) + len(CROSS))

    def z_copy(row, step):
        return pltpu.make_async_remote_copy(
            src_ref=rows.at[z], dst_ref=rows.at[row], send_sem=zs.at[along(step)], recv_sem=zr.at[row],
            device_id=(layer, feat_of(p, along(step))), device_id_type=MESH,
        )

    for step in Z_STEPS:
        z_copy(z, step).start()

    for dx in RING[:3]:
        to = plane_to(0, dx, 0)
        pl.semaphore_signal(ready.at[0], inc=1, device_id=(to[0], feat_of(to[1], z)), device_id_type=MESH)

    for copy in small[1:]:
        copy.wait()
    load_w.wait()
    scales = pow2(e_ref[0:1, :])
    for b in range(blocks):
        piece = slice(b * BLK, (b + 1) * BLK)
        w_v[piece, :] = (w_v[piece, :].astype(jnp.float32) * scales[0:1, b : b + 1]).astype(jnp.bfloat16)

    pl.semaphore_wait(ready.at[0], NX - 1)
    to = plane_to(0, 0, 1)
    pl.semaphore_signal(ready.at[1], inc=1, device_id=(to[0], feat), device_id_type=MESH)

    def p_copy(group, slot, other):
        return pltpu.make_async_remote_copy(
            src_ref=xgs[group].at[p], dst_ref=xgs[group].at[slot],
            send_sem=ps.at[group, other], recv_sem=pr.at[group, slot],
            device_id=(layer, feat_of(other, z)), device_id_type=MESH,
        )

    def spread(g):
        for i in range(SIZES[g]):
            row = STARTS[g] + i

            @pl.when(row != z)
            def _():
                z_copy(row, 1).wait_recv()

            stage[i * PITCH : i * PITCH + blocks, :] = rows[row].astype(jnp.float32)
        for b in range(blocks):
            xgs[g][p, :, b * BLK : (b + 1) * BLK] = stage[pl.ds(b, SIZES[g], stride=PITCH), :].astype(jnp.bfloat16)
        for dy in (1, 0):
            for dx in RING:
                if dy or dx:
                    p_copy(g, p, plane_to(dy, dx, 0)[1]).start()

    for g in GROUPS:
        spread(g)

    def l_copy(group, slot, other):
        return pltpu.make_async_remote_copy(
            src_ref=lat.at[layer, rows_of(group)], dst_ref=lat.at[slot, rows_of(group)],
            send_sem=ls.at[group, other], recv_sem=lr.at[group, slot],
            device_id=(other, feat), device_id_type=MESH,
        )


    def encode(g):
        @pl.loop(1, NP)
        def _(k):
            other = wrap(p + k, NP)
            p_copy(g, other, other).wait_recv()

        pre = jnp.dot(xgs[g][...].reshape(NP * SIZES[g], width), w_v[...], preferred_element_type=jnp.float32)
        lat[layer, rows_of(g)] = jnp.maximum(pre + eb_ref[...], 0.0).astype(jnp.bfloat16)
        for k in (2, 3, 1):
            l_copy(g, layer, wrap(layer + k, LY)).start()

    def r_copy(group, n):
        to = plane_to(*PLANE[n])
        return pltpu.make_async_remote_copy(
            src_ref=parts[group].at[to[0], to[1]], dst_ref=rs1s[group].at[layer, p],
            send_sem=rs_s.at[group, n], recv_sem=rs_r.at[group, n],
            device_id=(to[0], feat_of(to[1], z)), device_id_type=MESH,
        )

    def decode(g):
        @pl.loop(1, LY)
        def _(k):
            other = wrap(layer + k, LY)
            l_copy(g, other, other).wait_recv()

        for t in range(LY):
            first = t * (t + 1) // 2
            total = lax.dot_general(
                jnp.concatenate([lat[s, rows_of(g)] for s in range(t + 1)], axis=1),
                jnp.concatenate([d_v[first + s] for s in range(t + 1)], axis=1),
                (((1,), (1,)), ((), ())), preferred_element_type=jnp.float32,
            )
            parts[g][t, :, :, 0:cols] = total.reshape(NP, SIZES[g], cols).astype(jnp.bfloat16)
        for n in range(len(PLANE)):
            r_copy(g, n).start()
        rs1s[g][layer, p] = parts[g][layer, p]

    pl.semaphore_wait(ready.at[1], 1)
    for g in GROUPS:
        encode(g)
    load_d.wait()
    for g in GROUPS:
        decode(g)

    def f_copy(row, slot):
        return pltpu.make_async_remote_copy(
            src_ref=sb.at[row], dst_ref=rz.at[slot], send_sem=fs.at[row], recv_sem=fr.at[slot],
            device_id=(layer, feat_of(p, row)), device_id_type=MESH,
        )

    def gathered(g):
        for n in range(len(PLANE)):
            r_copy(g, n).wait_recv()

        for s in range(LY):
            total = rs1s[g][s, 0].astype(jnp.float32)
            for place in range(1, NP):
                total = total + rs1s[g][s, place].astype(jnp.float32)
            for c in range(chunks):
                stage2[pl.ds(s * chunks + c, SIZES[g], stride=PITCH), :] = total[:, c * BLK : (c + 1) * BLK]
        for i in range(SIZES[g]):
            sb[STARTS[g] + i] = stage2[i * PITCH : i * PITCH + LY * chunks, :].astype(jnp.bfloat16)

        for row in range(STARTS[g], STARTS[g] + SIZES[g]):

            @pl.when(row != z)
            def _():
                f_copy(row, z).start()

    for g in GROUPS:
        gathered(g)
    rz[z] = sb[z]

    @pl.loop(1, NZ)
    def _(k):
        other = wrap(z + k, NZ)
        f_copy(other, other).wait_recv()

    total = rz[0].astype(jnp.float32)
    for zz in range(1, NZ):
        total = total + rz[zz].astype(jnp.float32)

    half = BLK // 2
    low = lax.broadcasted_iota(jnp.int32, (1, BLK), 1) < half
    turned = pltpu.roll(total, half, 1)
    at = 0
    for pair in range(LY // 2):
        even, odd = pair * 2 * chunks, (pair * 2 + 1) * chunks
        pieces = [total[even + c : even + c + 1, :] for c in range(chunks - 1)]
        pieces.append(jnp.where(low, total[even + chunks - 1 : even + chunks, :], turned[odd : odd + 1, :]))
        for c in range(1, chunks):
            pieces.append(jnp.where(low, turned[odd + c - 1 : odd + c, :], turned[odd + c : odd + c + 1, :]))
        for piece in pieces:
            out_ref[0:1, at : at + BLK] = (piece + db_ref[0:1, at : at + BLK]).astype(jnp.bfloat16)
            at += BLK

    @pl.loop(1, NZ)
    def _(k):
        z_copy(z, k).wait_send()
        f_copy(wrap(z + k, NZ), z).wait_send()

    for g in GROUPS:
        @pl.loop(1, NP)
        def _(k):
            p_copy(g, p, wrap(p + k, NP)).wait_send()

        @pl.loop(1, LY)
        def _(k):
            l_copy(g, layer, wrap(layer + k, LY)).wait_send()

        for n in range(len(PLANE)):
            r_copy(g, n).wait_send()


def shards(resid_stream, enc_mantissa, enc_exponent, enc_bias, dec_weight, dec_bias):
    width = resid_stream.shape[2]
    feats = enc_mantissa.shape[2]
    pairs, _, cols = dec_weight.shape
    blocks = width // BLK
    padded = (cols + BLK - 1) // BLK * BLK
    vm = pl.BlockSpec(memory_space=pltpu.VMEM)
    hbm = pl.BlockSpec(memory_space=pl.ANY)
    dma = pltpu.SemaphoreType.DMA
    bf, f32 = jnp.bfloat16, jnp.float32
    out = pl.pallas_call(
        kernel,
        out_shape=jax.ShapeDtypeStruct((1, width), bf),
        in_specs=[hbm] * 6,
        out_specs=vm,
        scratch_shapes=[
            pltpu.VMEM((1, width), bf),
            pltpu.VMEM((1, blocks), jnp.int32),
            pltpu.VMEM((1, feats), f32),
            pltpu.VMEM((1, width), f32),
            pltpu.VMEM((width, feats), bf),
            pltpu.VMEM((pairs, cols, feats), bf),
            pltpu.VMEM((PITCH, BLK), f32),
            pltpu.VMEM((NZ, blocks, BLK), bf),
            pltpu.VMEM((max(SIZES) * PITCH, BLK), f32),
            [pltpu.VMEM((NP, size, width), bf) for size in SIZES],
            pltpu.VMEM((LY, NP * NZ, feats), bf),
            [pltpu.VMEM((LY, NP, size, padded), bf) for size in SIZES],
            [pltpu.VMEM((LY, NP, size, padded), bf) for size in SIZES],
            pltpu.VMEM((max(SIZES) * PITCH, BLK), f32),
            pltpu.VMEM((NZ, LY * padded // BLK, BLK), bf),
            pltpu.VMEM((NZ, LY * padded // BLK, BLK), bf),
            dma((6,)),
            pltpu.SemaphoreType.REGULAR((2,)),
            dma((NZ,)), dma((NZ,)),
            dma((len(SIZES), NP)), dma((len(SIZES), NP)),
            dma((len(SIZES), LY)), dma((len(SIZES), LY)),
            dma((len(SIZES), LY * NP)), dma((len(SIZES), LY * NP)),
            dma((NZ,)), dma((NZ,)),
        ],
        compiler_params=pltpu.CompilerParams(collective_id=0, has_side_effects=True),
    )(
        resid_stream.reshape(1, width),
        enc_mantissa[0],
        enc_exponent.reshape(1, blocks),
        enc_bias,
        dec_weight.transpose(0, 2, 1),
        dec_bias,
    )
    return out[:, None, :]


def solution(mesh):
    in_specs = (
        P("feat", "layer", None),
        P("layer", None, "feat"),
        P("layer", None, "feat"),
        P("layer", "feat"),
        P(None, "feat", "layer"),
        P("layer", None),
    )
    out_specs = P("feat", "layer", None)
    return jax.shard_map(shards, mesh=mesh, in_specs=in_specs, out_specs=out_specs, check_vma=False)
```
